128 devices in a mesh: prow: 8 (over x, core), pcol: 16 (over y, z).
Axes of the slice: x: 4, y: 4, z: 4, core: 2. Of those that a mesh axis runs over, the one named last changes fastest.
Arguments:
- front: float32 [16384, 16384], P('prow', 'pcol'), as said below
- parent_tile: int32 [64], replicated, may hold values from 0 to 63, as said below
Outputs:
- panel_factor: float32 [16384, 1024], P('prow')
- contribution: bfloat16 [16384, 16384], P('prow', 'pcol')
The draws below stay inside these ranges and needn't reach their ends.
Inputs may be any that keep to these rules, and one draw needn't show every extreme that they name: The front is symmetric positive definite in logical order, with smallest eigenvalue 0.5 or more. parent_tile is a permutation of the 64 tile indices. The tiles whose indices agree modulo 8 go to each such class of parent indices in groups of either none or exactly 2 tiles; tiles whose indices agree modulo 16 go to distinct classes of parent indices modulo 16.
All inputs are finite; a program needn't handle non-finite values.
Results may differ from the reference program's by a relative error of at most 0.001.
Values may be sent and summed in bfloat16 or wider, within the bound.
No kernel may reach another device: no remote copies, remote signals or barrier semaphores. Data moves between devices by JAX's collectives and lax.ppermute only.
A program may use at most 192 MiB of HBM per device.

```python
import jax
import jax.numpy as jnp
from jax import lax

TS = 256
TC = 4
PANELS = 2
PW = 2
NT = 64
TR = 8
NF = 16384
N_PROW = 8
N_PCOL = 16


def draw_front(key, part):
    count = TC * N_PCOL
    order = count * TS
    rows_dev = count // N_PROW
    inner = 2 * PANELS * PW * TS
    first, second = jax.random.split(jax.random.fold_in(key, 11), 2)
    raw = jax.random.normal(first, (order, inner), jnp.float32)
    diag_vals = jax.random.uniform(second, (order,), jnp.float32, 0.5, 2.0)
    product = jnp.dot(raw, raw.T, precision=lax.Precision.HIGHEST) * (4.0 / inner)
    product = 0.5 * (product + product.T)
    index = jnp.arange(order)
    matrix = product.at[index, index].add(diag_vals)
    matrix = matrix.reshape(rows_dev, N_PROW, TS, order).transpose(1, 0, 2, 3).reshape(order, order)
    matrix = matrix.reshape(order, TC, N_PCOL, TS).transpose(0, 2, 1, 3).reshape(order, order)
    return matrix.astype(jnp.float32)


def draw_parent_tile(key, part):
    first, second, third = jax.random.split(jax.random.fold_in(key, 23), 3)
    fourth = jax.random.fold_in(key, 29)
    group = N_PCOL // N_PROW
    sigma = jax.random.permutation(first, N_PROW)
    shifts = jax.random.permutation(second, N_PROW)[:TC]
    blocks = jax.random.permutation(third, TC)
    offset = jax.random.randint(fourth, (), 0, group)
    flips = (jnp.arange(TC) + offset) % group
    index = jnp.arange(TC * N_PCOL)
    slot = index // N_PCOL
    rest = index % N_PCOL
    upper = (rest // N_PROW + flips[slot]) % group
    lower = rest % N_PROW
    result = N_PCOL * blocks[slot] + N_PROW * upper + (sigma[lower] + shifts[slot]) % N_PROW
    return result.astype(jnp.int32)


def setup_inputs(seed: int = 0) -> dict:
    splits = jax.random.split(jax.random.key(seed), 3)
    front = draw_front(jax.random.fold_in(splits[2], 71), 0)
    parent_tile = draw_parent_tile(jax.random.fold_in(splits[2], 71), 0)
    return {"front": front, "parent_tile": parent_tile}


def to_logical(stored):
    rows = stored.reshape(N_PROW, TR, TS, NF).transpose(1, 0, 2, 3).reshape(NF, NF)
    return rows.reshape(NF, N_PCOL, TC, TS).transpose(0, 2, 1, 3).reshape(NF, NF)

def rows_stored(matrix):
    width = matrix.shape[1]
    return matrix.reshape(TR, N_PROW, TS, width).transpose(1, 0, 2, 3).reshape(NF, width)

def cols_stored(matrix):
    return matrix.reshape(NF, TC, N_PCOL, TS).transpose(0, 2, 1, 3).reshape(NF, NF)

def reference(front, parent_tile):
    steps_total = PANELS * PW
    work = to_logical(front)
    columns = []
    for step in range(steps_total):
        low = step * TS
        high = low + TS
        factor = jnp.linalg.cholesky(work[low:high, low:high])
        below = work[high:, low:high]
        solved = jax.scipy.linalg.solve_triangular(factor, below.T, lower=True).T
        columns.append(jnp.concatenate([jnp.zeros((low, TS), jnp.float32), factor, solved], axis=0))
        update = jnp.dot(solved, solved.T, precision=lax.Precision.HIGHEST)
        work = work.at[high:, high:].add(-update)
    panel_factor = rows_stored(jnp.concatenate(columns, axis=1))
    index = jnp.arange(NF, dtype=jnp.int32)
    keep = (index >= steps_total * TS)[:, None] & (index >= steps_total * TS)[None, :]
    schur = jnp.where(keep, work, 0.0).astype(jnp.bfloat16)
    tiles = jnp.arange(NT, dtype=jnp.int32)
    inverse = jnp.sum(jnp.where(parent_tile[None, :] == tiles[:, None], tiles[None, :], 0), axis=1).astype(jnp.int32)
    blocks = schur.reshape(NT, TS, NT, TS)
    moved = jnp.take(jnp.take(blocks, inverse, axis=0), inverse, axis=2).reshape(NF, NF)
    contribution = cols_stored(rows_stored(moved))
    return (panel_factor, contribution)
```

```python
import functools

import jax
import jax.numpy as jnp
from jax import lax
from jax.experimental import pallas as pl
from jax.experimental.pallas import tpu as pltpu
from jax.sharding import PartitionSpec as P

TS = 256
KT = 4
HB = 128
ALL = ("prow", "pcol")
LOWER = [(i, j) for i in range(KT) for j in range(i + 1)]
AT = {ij: n for n, ij in enumerate(LOWER)}
NN = (((1,), (0,)), ((), ()))
NTD = (((1,), (1,)), ((), ()))
f32 = jnp.float32
bf16 = jnp.bfloat16


def fdot(a, b, dims):
    return lax.dot_general(
        a, b, dims, precision=lax.Precision.HIGHEST, preferred_element_type=f32
    )


def split(x):
    hi = x.astype(bf16)
    return hi, (x - hi.astype(f32)).astype(bf16)


def bdot(a, b, dims):
    return lax.dot_general(a, b, dims, preferred_element_type=f32)


def dot3(a, b, dims):
    return bdot(a[0], b[0], dims) + (bdot(a[0], b[1], dims) + bdot(a[1], b[0], dims))


def base_inverse(src, dst):
    n = HB // 8
    sub = lax.broadcasted_iota(jnp.int32, (8, HB), 0)
    lane = lax.broadcasted_iota(jnp.int32, (8, HB), 1)
    a = [src[8 * i : 8 * i + 8, :] for i in range(n)]
    b = [jnp.where(lane == sub + 8 * i, 1.0, 0.0).astype(f32) for i in range(n)]
    for g in range(n):
        cols = [jnp.broadcast_to(a[g][:, 8 * g + k : 8 * g + k + 1], (8, HB)) for k in range(8)]
        row, brow = a[g], b[g]
        rows, brows, recips, coefs = [], [], [], []
        scale = jnp.zeros((8, HB), f32)
        for j in range(8):
            pivot = cols[j][j : j + 1, :]
            recip = 1.0 / pivot
            scale = jnp.where(sub == j, pivot, scale)
            coef = [cols[k][j : j + 1, :] for k in range(8)]
            factor = jnp.where(sub > j, cols[j] * recip, 0.0)
            rows.append(row[j : j + 1, :])
            brows.append(brow[j : j + 1, :])
            recips.append(recip)
            coefs.append(coef)
            for k in range(j + 1, 8):
                cols[k] = cols[k] - factor * coef[k]
            row = row - factor * rows[j]
            brow = brow - factor * brows[j]
        for i in range(g + 1, n):
            below = [
                jnp.broadcast_to(a[i][:, 8 * g + k : 8 * g + k + 1], (8, HB)) for k in range(8)
            ]
            for j in range(8):
                factor = below[j] * recips[j]
                for k in range(j + 1, 8):
                    below[k] = below[k] - factor * coefs[j][k]
                a[i] = a[i] - factor * rows[j]
                b[i] = b[i] - factor * brows[j]
        dst[8 * g : 8 * g + 8, :] = jnp.where(lane <= sub + 8 * g, brow * lax.rsqrt(scale), 0.0)


def chain_kernel(d_ref, hi_ref, lo_ref, work, cur, inv, first, left, mixed):
    work[...] = d_ref[...]
    cur[...] = d_ref[0, :HB, :HB]

    def put(ij, value):
        hi, lo = split(value)
        hi_ref[AT[ij]] = hi
        lo_ref[AT[ij]] = lo

    def body(step, carry):
        base_inverse(cur, inv)
        for k in range(KT):

            @pl.when(step == 2 * k)
            def _():
                tile = AT[k, k]
                first[...] = inv[...]
                low = fdot(work[tile, HB:, :HB], inv[...], NTD)
                cur[...] = work[tile, HB:, HB:] - fdot(low, low, NTD)
                mixed[...] = fdot(low, inv[...], NN)

            @pl.when(step == 2 * k + 1)
            def _():
                corner = -fdot(inv[...], mixed[...], NN)
                whole = jnp.concatenate(
                    [
                        jnp.concatenate([first[...], jnp.zeros((HB, HB), f32)], axis=1),
                        jnp.concatenate([corner, inv[...]], axis=1),
                    ],
                    axis=0,
                )
                put((k, k), whole)
                for i in range(k + 1, KT):
                    solved = fdot(work[AT[i, k]], whole, NTD)
                    left[i] = solved
                    put((i, k), solved)
                    for j in range(k + 1, i + 1):
                        tile = AT[i, j]
                        work[tile] = work[tile] - fdot(left[i], left[j], NTD)
                if k + 1 < KT:
                    cur[...] = work[AT[k + 1, k + 1], :HB, :HB]

        return carry

    lax.fori_loop(0, 2 * KT, body, 0)


def chain(diag):
    shape = jax.ShapeDtypeStruct((len(LOWER), TS, TS), bf16)
    vmem = pl.BlockSpec(memory_space=pltpu.VMEM)
    return pl.pallas_call(
        chain_kernel,
        out_shape=(shape, shape),
        in_specs=[vmem],
        out_specs=(vmem, vmem),
        scratch_shapes=[
            pltpu.VMEM((len(LOWER), TS, TS), f32),
            pltpu.VMEM((HB, HB), f32),
            pltpu.VMEM((HB, HB), f32),
            pltpu.VMEM((HB, HB), f32),
            pltpu.VMEM((KT, TS, TS), f32),
            pltpu.VMEM((HB, HB), f32),
        ],
        cost_estimate=pl.CostEstimate(flops=10**9, bytes_accessed=5 * 2**20, transcendentals=0),
        name="chain",
    )(diag)


def rows_kernel(
    place, hi_ref, lo_ref, u_ref, a_ref, f_ref, mix_ref, l_ref, s_ref, vhi, vlo, *, tc, part
):
    step = pl.program_id(0)
    width = tc * TS

    def low(i, j):
        return hi_ref[AT[i, j]], lo_ref[AT[i, j]]

    @pl.when(step == 0)
    def _():
        for k in range(KT):
            strip = jnp.concatenate([u_ref[0, k], u_ref[1, k]], axis=0)
            for j in range(k):
                top = slice(j * TS, (j + 1) * TS)
                strip = strip - dot3(low(k, j), (vhi[top, :], vlo[top, :]), NN)
            hi, lo = split(dot3(low(k, k), split(strip), NN))
            vhi[k * TS : (k + 1) * TS, :] = hi
            vlo[k * TS : (k + 1) * TS, :] = lo

    tr = f_ref.shape[0]
    rows = tr * part
    solved, pieces = [], []
    for k in range(KT):
        col = a_ref[:, k].reshape(rows, TS)
        for j in range(k):
            col = col - dot3(solved[j], low(k, j), NTD)
        value = dot3(split(col), low(k, k), NTD)
        line = lax.broadcasted_iota(jnp.int32, (tr, part, TS), 1) + step * part
        slot = lax.broadcasted_iota(jnp.int32, (tr, part, TS), 0) * place[2] + place[0]
        across = lax.broadcasted_iota(jnp.int32, (tr, part, TS), 2) + k * TS
        keep = across <= slot * TS + line
        value = jnp.where(keep, value.reshape(tr, part, TS), 0.0)
        l_ref[:, :, k * TS : (k + 1) * TS] = value
        hi, lo = split(value.reshape(rows, TS))
        solved.append((hi, lo))
    lhi = jnp.concatenate([s[0] for s in solved], axis=1)
    llo = jnp.concatenate([s[1] for s in solved], axis=1)
    prod = dot3((lhi, llo), (vhi[...], vlo[...]), NN)
    full = f_ref[...] - prod.reshape(tr, part, width)
    slot = lax.broadcasted_iota(jnp.int32, full.shape, 0) * place[2] + place[0]
    across = lax.broadcasted_iota(jnp.int32, full.shape, 2) // TS * place[3] + place[1]
    full = jnp.where((slot >= KT) & (across >= KT), full, 0.0).astype(bf16)
    for g in range(part // 16):
        block = full[:, 16 * g : 16 * g + 16, :].reshape(tr * 16, width)
        s_ref[g * tr * 16 : (g + 1) * tr * 16, :] = bdot(mix_ref[...], block, NN).astype(bf16)


def solve_rows(place, hi, lo, u, a, front, mix, part):
    tr, tc = front.shape[0] // TS, front.shape[1] // TS
    tiles = front.reshape(tr, TS, tc * TS)
    whole = lambda shape: pl.BlockSpec(
        shape, lambda g: (0,) * len(shape), pipeline_mode=pl.Buffered(1)
    )
    cut = pl.BlockSpec((tr, part, tc * TS), lambda g: (0, g, 0))
    return pl.pallas_call(
        functools.partial(rows_kernel, tc=tc, part=part),
        grid=(TS // part,),
        in_specs=[
            pl.BlockSpec(memory_space=pltpu.SMEM),
            whole(hi.shape),
            whole(lo.shape),
            whole(u.shape),
            pl.BlockSpec(a.shape[:3] + (part, TS), lambda g: (0, 0, 0, g, 0)),
            cut,
            whole(mix.shape),
        ],
        out_specs=(
            pl.BlockSpec((tr, part, KT * TS), lambda g: (0, g, 0)),
            pl.BlockSpec((tr * part, tc * TS), lambda g: (g, 0)),
        ),
        out_shape=(
            jax.ShapeDtypeStruct((tr, TS, KT * TS), f32),
            jax.ShapeDtypeStruct((tr * TS, tc * TS), bf16),
        ),
        scratch_shapes=[
            pltpu.VMEM((KT * TS, tc * TS), bf16),
            pltpu.VMEM((KT * TS, tc * TS), bf16),
        ],
        compiler_params=pltpu.CompilerParams(vmem_limit_bytes=60 * 2**20),
        name="solve_rows",
    )(place, hi, lo, u, a, tiles, mix)


def middle_kernel(inv_ref, x_ref, p_ref, y_ref, *, cols):
    here = pl.program_id(0)
    tr = x_ref.shape[0]
    tc = x_ref.shape[3] // TS
    for m in range(tc):
        child = inv_ref[m * cols + here]
        lanes = pl.ds(pl.multiple_of(child // cols * TS, TS), TS)
        block = x_ref[:, child % cols, :, lanes].reshape(tr * 16, TS)
        moved = bdot(p_ref[...], block, NN).astype(bf16)
        y_ref[:, 0, :, m * TS : (m + 1) * TS] = moved.reshape(tr, 16, TS)


def middle(inverse, x, perm):
    tr, cols, _, width = x.shape
    return pl.pallas_call(
        functools.partial(middle_kernel, cols=cols),
        grid_spec=pltpu.PrefetchScalarGridSpec(
            num_scalar_prefetch=1,
            grid=(cols,),
            in_specs=[
                pl.BlockSpec(x.shape, lambda c, inv: (0, 0, 0, 0), pipeline_mode=pl.Buffered(1)),
                pl.BlockSpec(perm.shape, lambda c, inv: (0, 0)),
            ],
            out_specs=pl.BlockSpec((tr, 1, 16, width), lambda c, inv: (0, c, 0, 0)),
        ),
        out_shape=jax.ShapeDtypeStruct(x.shape, bf16),
        name="middle",
    )(inverse, x, perm)


def last_kernel(z_ref, p_ref, c_ref):
    block = z_ref[...]
    count, depth, width = block.shape
    moved = bdot(p_ref[...], block.reshape(count * depth, width), NN).astype(bf16)
    c_ref[...] = moved.reshape(c_ref.shape)


def last(z, unmix, tr):
    width = z.shape[2]
    return pl.pallas_call(
        last_kernel,
        grid=(TS // 16,),
        in_specs=[
            pl.BlockSpec((8, 16, width), lambda g: (g, 0, 0)),
            pl.BlockSpec(unmix.shape, lambda g: (0, 0)),
        ],
        out_specs=pl.BlockSpec((tr, 16, width), lambda g: (0, g, 0)),
        out_shape=jax.ShapeDtypeStruct((tr, TS, width), bf16),
        name="last",
    )(z, unmix)


def shards(front, parent_tile):
    prows = lax.axis_size("prow")
    pcols = lax.axis_size("pcol")
    row_id = lax.axis_index("prow")
    col_id = lax.axis_index("pcol")
    devices = prows * pcols
    tr = front.shape[0] // TS
    tc = front.shape[1] // TS
    per = TS // devices

    corner = front[:TS, :TS].reshape(devices, per, TS)
    spread = lax.all_to_all(corner, ALL, 0, 0, tiled=True)
    mine = jnp.stack([spread[i * pcols + j] for i, j in LOWER])
    sent = jnp.broadcast_to(mine[None], (devices,) + mine.shape)
    got = lax.all_to_all(sent, ALL, 0, 0, tiled=True)
    diag = got.transpose(1, 0, 2, 3).reshape(len(LOWER), TS, TS)

    group = pcols // KT
    lead = front[:, :TS].reshape(group, tr // group * TS, TS)
    shard = lead[0]
    for y in range(1, group):
        part = lax.ppermute(lead[y], "pcol", [(j, j + KT * y) for j in range(KT)])
        shard = jnp.where(col_id // KT == y, part, shard)
    panel = lax.all_gather(shard, "pcol", axis=0, tiled=False)
    panel = panel.reshape(group, KT, tr // group, TS, TS)

    head = front[:TS].reshape(2, HB, tc * TS)
    part = lax.ppermute(head[1], "prow", [(k, k + KT) for k in range(KT)])
    part = jnp.where(row_id < KT, head[0], part)
    strips = lax.all_gather(part, "prow", axis=0, tiled=False).reshape(2, KT, HB, tc * TS)

    total = parent_tile.shape[0]
    every = jnp.arange(total, dtype=jnp.int32)
    inverse = jnp.sum(jnp.where(parent_tile[None, :] == every[:, None], every[None, :], 0), axis=1)
    inverse = inverse.astype(jnp.int32)
    line = jnp.arange(tr * 16, dtype=jnp.int32)
    child = inverse.reshape(tr, prows).T.reshape(-1)
    source = (child % prows) * tr + child // prows
    pick = jnp.repeat(source, 2) * 2 + line % 2
    perm = (pick[:, None] == line[None, :]).astype(bf16)
    mixed = line % 16 // 2 * 16 + line // 16 * 2 + line % 2
    mix = (mixed[:, None] == line[None, :]).astype(bf16)

    hi, lo = chain(diag)
    place = jnp.stack([row_id, col_id, jnp.int32(prows), jnp.int32(pcols)]).astype(jnp.int32)
    panel_factor, schur = solve_rows(place, hi, lo, strips, panel, front, mix, 64)
    panel_factor = panel_factor.reshape(tr * TS, KT * TS)

    first = lax.all_to_all(
        schur.reshape(devices, tr * per, tc * TS), ALL, 0, 0, tiled=True
    )
    moved = middle(inverse, first.reshape(prows, pcols, tr * per, tc * TS), perm)
    second = lax.all_to_all(
        moved.reshape(devices, tr * per, tc * TS), ALL, 0, 0, tiled=True
    )
    contribution = last(second, mix, tr).reshape(tr * TS, tc * TS)
    return (panel_factor, contribution)


def solution(mesh):
    return jax.shard_map(
        shards,
        mesh=mesh,
        in_specs=(P("prow", "pcol"), P()),
        out_specs=(P("prow", None), P("prow", "pcol")),
        check_vma=False,
    )
```
